512 devices in a mesh: ctx: 64 (over y_hi, z, core), tp: 8 (over x, y_lo).
Axes of the slice: x: 4, y: 8 (y_hi: 4, y_lo: 2; y = y_hi * 2 + y_lo), z: 8, core: 2. Of those that a mesh axis runs over, the one named last changes fastest.
Arguments:
- q_new: bfloat16 [1024, 8192], P(('ctx', 'tp')), may hold values from -128 to 128
- kv_new: bfloat16 [2, 1024, 1024], P(None, 'ctx', 'tp'), may hold values from -4 to 4
- kv_cache: bfloat16 [2, 31744, 1024], P(None, 'ctx', 'tp'), may hold values from -4 to 4
- cache_lens: int32 [64], replicated, may hold values from 1 to 496, 15872 in all
- segment_ids: int32 [1024], replicated, may hold values from 0 to 63, never falling along the last dimension, each value on 1 to 32 neighbouring positions
Outputs:
- attn_out: bfloat16 [1024, 8192], P(('ctx', 'tp'))
- attn_lse: float32 [1024, 64], P('ctx', 'tp')
The draws below stay inside these ranges and needn't reach their ends.
Inputs may be any that keep to these rules, and one draw needn't show every extreme that they name: The filled slots of shard c are its first cache_lens[c] slots; the lengths sum to 15872 and some shard is full. `segment_ids`: never falls along the turn; a segment holds at most 32 tokens, and some segment exactly 32.
All inputs are finite; a program needn't handle non-finite values.
Results may differ from the reference program's by a relative error of at most 0.0015.
Values may be sent and summed in bfloat16 or wider, within the bound.
No kernel may reach another device: no remote copies, remote signals or barrier semaphores. Data moves between devices by JAX's collectives and lax.ppermute only.
A program may use at most 64 MiB of HBM per device.

```python
import math
import jax
import jax.numpy as jnp
import numpy as np
from jax import lax

HD = 128
GROUP = 8
CACHE_DEV = 496
QB = 16
KVH = 8
HQ = 64
CACHE = 31744
NEW = 1024
N_CTX = 64


def cache_base(key):
    stream = jax.random.fold_in(key, 17)
    base = jnp.clip(jax.random.normal(stream, (2, CACHE, KVH * HD), jnp.float32), -4.0, 4.0)
    return base


def draw_kv_cache(key, part):
    return cache_base(key).astype(jnp.bfloat16)


def draw_q_new(key, part):
    stream = jax.random.fold_in(key, 29)
    base = jnp.clip(3.0 * jax.random.normal(stream, (NEW, HQ * HD), jnp.float32), -18.0, 18.0)
    return base.astype(jnp.bfloat16)


def levels(own_key, dims, cuts, smallest, top_value):
    def one(axis_at, shards_of):
        draws = jax.random.uniform(jax.random.fold_in(jax.random.fold_in(own_key, 6), axis_at), (shards_of,), jnp.float32, smallest / len(cuts), top_value / len(cuts))
        return jnp.repeat(jnp.exp(draws), dims[axis_at] // shards_of).reshape((-1,) + (1,) * (len(dims) - axis_at - 1))

    level = one(*cuts[0])
    for cut in cuts[1:]:
        level = level * one(*cut)
    return level


def length_profile(amount, total, reach, slope):
    weights = [(1 << 20) // math.isqrt(standing ** slope) + 1 for standing in range(2, amount + 1)]
    rest, holding = total - reach - (amount - 1), [1] * (amount - 1)
    while rest > 0:
        free = [i for i in range(amount - 1) if holding[i] < reach]
        whole, budget = sum([weights[i] for i in free]), rest
        for i in free:
            addition = min(reach - holding[i], max(1, budget * weights[i] // whole), rest)
            holding[i] = holding[i] + addition
            rest = rest - addition
    return np.array([reach] + holding)


def uneven_parts(key, amount, total, reach, slope):
    if amount == 2:
        one = jax.random.randint(key, (), max(1, total - reach), min(reach, total - 1) + 1)
        return jnp.stack([one, total - one])
    sizes = jnp.asarray(length_profile(amount, total, reach, slope), jnp.int32)
    couples = (amount - 1) // 2
    source_of, taker = sizes[1:1 + 2 * couples:2], sizes[2:2 + 2 * couples:2]
    room = jnp.minimum(source_of - 1, reach - taker)
    shifted = jax.random.randint(jax.random.fold_in(key, 1), (couples,), 0, 1 << 20) % (room + 1)
    sizes = sizes.at[1:1 + 2 * couples:2].set(source_of - shifted).at[2:2 + 2 * couples:2].set(taker + shifted)
    return sizes[jax.random.permutation(jax.random.fold_in(key, 2), amount)]


def bell_draw(rng, dims, spread, bound, split=(), kind=jnp.bfloat16):
    entries = jax.random.normal(rng, dims, jnp.float32) * spread
    if len(split) > 0:
        entries = levels(rng, dims, split, -0.22, 0.18) * entries
    return jnp.clip(entries, min=-bound, max=bound).astype(kind)


def setup_inputs(seed: int = 0) -> dict:
    splits = jax.random.split(jax.random.key(seed), 6)
    q_new = draw_q_new(jax.random.fold_in(splits[5], 71), 0)
    kv_new = bell_draw(splits[1], (2, NEW, KVH * HD), 1.0, 4.0, ((1, 64), (2, 8)))
    kv_cache = draw_kv_cache(jax.random.fold_in(splits[5], 71), 0)
    cache_lens = uneven_parts(splits[3], N_CTX, CACHE // 2, CACHE_DEV, 2).astype(jnp.int32)
    segment_ids = jnp.searchsorted(jnp.cumsum(uneven_parts(splits[4], NEW // 16, NEW, 32, 2)), jnp.arange(NEW), side="right").astype(jnp.int32)
    return {"q_new": q_new, "kv_new": kv_new, "kv_cache": kv_cache, "cache_lens": cache_lens, "segment_ids": segment_ids}


def shard_partial(queries, query_seg, keys_all, values_all, filled, key_seg, head_dim):
    rows = queries.shape[0]
    heads = queries.shape[1] // head_dim
    total = keys_all.shape[0]
    cache_count = total - key_seg.shape[0]
    flat = queries.reshape(rows * heads, head_dim)
    scores = jnp.dot(flat, keys_all.T, preferred_element_type=jnp.float32) * (head_dim ** -0.5)
    scores = scores.reshape(rows, heads, total)
    slot_rank = jnp.where(jnp.arange(cache_count) < filled, -1, 2 ** 30).astype(jnp.int32)
    key_rank = jnp.concatenate([slot_rank, key_seg.astype(jnp.int32)])
    visible = key_rank[None, None, :] <= query_seg.astype(jnp.int32)[:, None, None]
    masked = jnp.where(visible, scores, -jnp.inf)
    peak = jnp.max(masked, axis=2)
    expo = jnp.exp(masked - peak[:, :, None])
    denom = jnp.sum(expo, axis=2)
    weights = expo.astype(jnp.bfloat16).reshape(rows * heads, total)
    mixed = jnp.dot(weights, values_all, preferred_element_type=jnp.float32)
    mixed = mixed.reshape(rows, heads, head_dim) / denom[:, :, None]
    return mixed.reshape(rows, heads * head_dim), peak + jnp.log(denom)


def reference(q_new, kv_new, kv_cache, cache_lens, segment_ids):
    outputs = []
    totals = []
    for group in range(KVH):
        lo = group * HD
        queries = q_new[:, group * GROUP * HD:(group + 1) * GROUP * HD]
        cache_keys = kv_cache[0, :, lo:lo + HD]
        cache_values = kv_cache[1, :, lo:lo + HD]
        new_keys = kv_new[0, :, lo:lo + HD]
        new_values = kv_new[1, :, lo:lo + HD]

        def visit(carry, shard):
            peak_run, denom_run, numer_run = carry
            start = (shard * CACHE_DEV).astype(jnp.int32)
            begin = (shard * QB).astype(jnp.int32)
            keys_all = jnp.concatenate([lax.dynamic_slice_in_dim(cache_keys, start, CACHE_DEV, 0), lax.dynamic_slice_in_dim(new_keys, begin, QB, 0)])
            values_all = jnp.concatenate([lax.dynamic_slice_in_dim(cache_values, start, CACHE_DEV, 0), lax.dynamic_slice_in_dim(new_values, begin, QB, 0)])
            key_seg = lax.dynamic_slice_in_dim(segment_ids, begin, QB, 0)
            mixed, lse = shard_partial(queries, segment_ids, keys_all, values_all, cache_lens[shard], key_seg, HD)
            peak = jnp.maximum(peak_run, lse)
            keep = jnp.exp(peak_run - peak)
            fresh = jnp.exp(lse - peak)
            numer = numer_run * keep[:, :, None] + mixed.reshape(NEW, GROUP, HD) * fresh[:, :, None]
            return (peak, denom_run * keep + fresh, numer), None

        init = (jnp.full((NEW, GROUP), -jnp.inf, jnp.float32), jnp.zeros((NEW, GROUP), jnp.float32), jnp.zeros((NEW, GROUP, HD), jnp.float32))
        (peak, denom, numer), _ = lax.scan(visit, init, jnp.arange(N_CTX, dtype=jnp.int32))
        outputs.append((numer / denom[:, :, None]).reshape(NEW, GROUP * HD).astype(jnp.bfloat16))
        totals.append(peak + jnp.log(denom))
    return jnp.concatenate(outputs, axis=1), jnp.concatenate(totals, axis=1)
```

```python
import functools
import math

import jax
import jax.numpy as jnp
from jax import lax
from jax.experimental import pallas as pl
from jax.experimental.pallas import tpu as pltpu
from jax.sharding import Mesh
from jax.sharding import PartitionSpec as P

HEAD = 128
NEG = float("-inf")
CTX = ("yh", "z", "core")
TP = ("x", "yl")
ROUTE = ("z", "x", "yl")


def prep_kernel(lens_ref, ids_ref, place_ref, filled_ref, kseg_ref, qseg_ref):
    yh, z, core = place_ref[0], place_ref[1], place_ref[2]
    row = lax.broadcasted_iota(jnp.int32, (16, 256), 0)
    token = lax.broadcasted_iota(jnp.int32, (8, 128), 1) // 8
    which = lax.broadcasted_iota(jnp.int32, (8, 128), 0)
    filled = jnp.zeros((8, 128), jnp.int32)
    for j in range(8):
        shard = ((yh + 4 - j // 2) % 4) * 16 + z * 2 + (core + j % 2) % 2
        filled = jnp.where(which == j, lens_ref[shard], filled)
        seg = jnp.zeros((16, 256), jnp.int32)
        for i in range(16):
            seg = jnp.where(row == i, ids_ref[shard * 16 + i], seg)
        kseg_ref[j] = seg
    filled_ref[...] = filled
    for zz in range(8):
        first = (yh * 16 + zz * 2 + core) * 16
        seg = jnp.zeros((8, 128), jnp.int32)
        for i in range(16):
            seg = jnp.where(token == i, ids_ref[first + i], seg)
        qseg_ref[:, zz * 128 : (zz + 1) * 128] = seg


def prep(lens, ids, place):
    smem = pl.BlockSpec(memory_space=pltpu.SMEM)
    vmem = pl.BlockSpec(memory_space=pltpu.VMEM)
    return pl.pallas_call(
        prep_kernel,
        out_shape=(
            jax.ShapeDtypeStruct((8, 128), jnp.int32),
            jax.ShapeDtypeStruct((8, 16, 256), jnp.int32),
            jax.ShapeDtypeStruct((8, 1024), jnp.int32),
        ),
        in_specs=[smem, smem, smem],
        out_specs=(vmem, vmem, vmem),
        name="prep",
    )(lens, ids, place)


def attend_kernel(shards, has_state, final, *refs):
    q_ref, filled_ref, kseg_ref, qseg_ref = refs[:4]
    chunk_refs = refs[4 : 4 + len(shards)]
    rest = refs[4 + len(shards) :]
    state_ref = rest[0] if has_state else None
    out_ref = rest[-1]
    rows = q_ref.shape[0]
    total = chunk_refs[0].shape[1]
    cache = total - 16
    tile = 256
    scale = HEAD**-0.5
    factor = scale * math.log2(math.e)
    slot = lax.broadcasted_iota(jnp.int32, (cache, 128), 0)
    for part in range(rows // tile):
        cols = slice(part * tile, (part + 1) * tile)
        q = q_ref[cols, :]
        qseg = qseg_ref[0:1, cols]
        if has_state:
            acc = state_ref[0:HEAD, cols]
            peak = state_ref[HEAD : HEAD + 1, cols]
            denom = state_ref[HEAD + 1 : HEAD + 2, cols]
        else:
            acc = peak = denom = None
        for which, j in enumerate(shards):
            keys = chunk_refs[which][0]
            values = chunk_refs[which][1]
            s = lax.dot_general(keys, q, (((1,), (1,)), ((), ())), preferred_element_type=jnp.float32)
            bias = jnp.where(slot < filled_ref[j : j + 1, :], 0.0, NEG).astype(jnp.float32)
            old = s[:cache] + jnp.concatenate([bias, bias], axis=1)
            new = jnp.where(kseg_ref[j] <= qseg, s[cache:], NEG)
            m = jnp.maximum(jnp.max(old, axis=0, keepdims=True), jnp.max(new, axis=0, keepdims=True))
            old = jnp.exp2((old - m) * factor)
            new = jnp.exp2((new - m) * factor)
            l = jnp.sum(old, axis=0, keepdims=True) + jnp.sum(new, axis=0, keepdims=True)
            w = jnp.concatenate([old.astype(jnp.bfloat16), new.astype(jnp.bfloat16)], axis=0)
            o = lax.dot_general(values, w, (((0,), (0,)), ((), ())), preferred_element_type=jnp.float32)
            if acc is None:
                acc, peak, denom = o, m, l
            else:
                top = jnp.maximum(peak, m)
                keep = jnp.exp2((peak - top) * factor)
                fresh = jnp.exp2((m - top) * factor)
                acc = acc * keep + o * fresh
                denom = denom * keep + l * fresh
                peak = top
        if not final:
            out_ref[0:HEAD, cols] = acc
            out_ref[HEAD : HEAD + 1, cols] = peak
            out_ref[HEAD + 1 : HEAD + 2, cols] = denom
        else:
            acc = acc / denom
            lse = peak * scale + jnp.log(denom)
            for half in range(tile // 128):
                block = acc[:, half * 128 : (half + 1) * 128].T
                line = lse[:, half * 128 : (half + 1) * 128]
                for t in range(8):
                    at = ((part * (tile // 128) + half) * 8 + t) * 17
                    out_ref[at : at + 16, :] = block[t * 16 : (t + 1) * 16, :]
                    out_ref[at + 16 : at + 17, :] = line


def attend(shards, q, prepared, chunks, state=None, final=False):
    vmem = pl.BlockSpec(memory_space=pltpu.VMEM)
    operands = [q, *prepared, *chunks]
    aliases = {}
    shape = (1088, 128) if final else (HEAD + 8, q.shape[0])
    if state is not None:
        if not final:
            aliases = {len(operands): 0}
        operands.append(state)
    work = len(shards) * q.shape[0] * chunks[0].shape[1]
    return pl.pallas_call(
        functools.partial(attend_kernel, tuple(shards), state is not None, final),
        out_shape=jax.ShapeDtypeStruct(shape, jnp.float32),
        in_specs=[vmem] * len(operands),
        out_specs=vmem,
        input_output_aliases=aliases,
        cost_estimate=pl.CostEstimate(flops=4 * HEAD * work, transcendentals=work, bytes_accessed=1 << 20),
        compiler_params=pltpu.CompilerParams(vmem_limit_bytes=32 << 20),
        name="attend",
    )(*operands)


def combine_kernel(place_ref, got_ref, out_ref, lse_ref, turned_ref, line_ref):
    me = place_ref[3]
    lse = got_ref[pl.ds(16, 64, stride=17), :].reshape(8, 8, 128)
    peak = jnp.max(lse, axis=0)
    w = jnp.exp(lse - peak[None])
    denom = jnp.sum(w, axis=0)
    w = (w / denom[None]).reshape(64, 128)
    turned_ref[...] = jnp.concatenate([w, w], axis=0).T
    line_ref[...] = peak + jnp.log(denom)
    mine = turned_ref[pl.ds(pl.multiple_of(me * 16, 16), 16), :]
    for g in range(8):
        acc = None
        for z in range(8):
            at = z * 8 + g
            term = got_ref[at * 17 : at * 17 + 16, :] * mine[:, at : at + 1]
            acc = term if acc is None else acc + term
        acc = acc.astype(jnp.bfloat16)
        out_ref[0, g * 8 : (g + 1) * 8, :] = acc[:8]
        out_ref[1, g * 8 : (g + 1) * 8, :] = acc[8:]
    line = jnp.broadcast_to(line_ref[pl.ds(me, 1), :], (16, 128))
    row = lax.broadcasted_iota(jnp.int32, (16, 128), 0)
    table = line
    for i in range(1, 16):
        table = jnp.where(row == i, pltpu.roll(line, 128 - 8 * i, 1), table)
    lse_ref[...] = table[:, :8]


def combine(place, got):
    smem = pl.BlockSpec(memory_space=pltpu.SMEM)
    vmem = pl.BlockSpec(memory_space=pltpu.VMEM)
    return pl.pallas_call(
        combine_kernel,
        out_shape=(
            jax.ShapeDtypeStruct((2, 64, 128), jnp.bfloat16),
            jax.ShapeDtypeStruct((16, 8), jnp.float32),
        ),
        in_specs=[smem, vmem],
        out_specs=(vmem, vmem),
        scratch_shapes=[pltpu.VMEM((128, 128), jnp.float32), pltpu.VMEM((8, 128), jnp.float32)],
        name="combine",
    )(place, got)


def shards_program(q_new, kv_new, kv_cache, cache_lens, segment_ids):
    place = jnp.stack(
        [lax.axis_index("yh"), lax.axis_index("z"), lax.axis_index("core"), lax.axis_index(TP)]
    ).astype(jnp.int32)
    across = [(0, 1), (1, 0)]

    def shift(x, by):
        return lax.ppermute(x, "yh", [(i, (i + by) % 4) for i in range(4)])

    own = jnp.concatenate([kv_cache, kv_new], axis=1)
    one = shift(own, 1)
    three = shift(own, 3)
    two = shift(own, 2)
    q = q_new.reshape(2, 8, 8, HEAD).transpose(1, 0, 2, 3).reshape(1, 8, 16, HEAD)
    q = jnp.broadcast_to(q, (8, 8, 16, HEAD)).reshape(64, 16, HEAD)
    q = lax.all_to_all(q, ROUTE, split_axis=0, concat_axis=0, tiled=True).reshape(1024, HEAD)
    prepared = prep(cache_lens, segment_ids, place)
    own_x = lax.ppermute(own, "core", across)
    state = attend([0, 1], q, prepared, [own, own_x])
    one_x = lax.ppermute(one, "core", across)
    state = attend([2, 3], q, prepared, [one, one_x], state)
    three_x = lax.ppermute(three, "core", across)
    state = attend([6, 7], q, prepared, [three, three_x], state)
    two_x = lax.ppermute(two, "core", across)
    state = attend([4], q, prepared, [two], state)
    sent = attend([5], q, prepared, [two_x], state, final=True)
    got = lax.all_to_all(sent.reshape(64, 1, 2176), ROUTE, split_axis=0, concat_axis=0, tiled=True)
    out, lse = combine(place, got.reshape(1088, HEAD))
    return out.reshape(2, 8192), lse


def solution(mesh):
    fine = Mesh(mesh.devices.reshape(4, 8, 2, 4, 2), CTX + TP)
    rows = P(CTX + TP, None)
    kv = P(None, CTX, TP)
    return jax.shard_map(
        shards_program,
        mesh=fine,
        in_specs=(rows, kv, kv, P(), P()),
        out_specs=(rows, P(CTX, TP)),
        check_vma=False,
    )
```

```python
import functools
import math

import jax
import jax.numpy as jnp
from jax import lax
from jax.experimental import pallas as pl
from jax.experimental.pallas import tpu as pltpu
from jax.sharding import Mesh
from jax.sharding import PartitionSpec as P


HEAD = 128
HIDE = -1e30
CTX = ("y1", "y0", "z1", "z0", "core")
TP = ("x", "yl")
ROUTE = ("z1", "z0", "x", "yl")


def prep_kernel(lens_ref, ids_ref, place_ref, hide_ref, pick_ref):
    block = pick_ref.shape[0] // 64
    y, z, core = place_ref[1], place_ref[2], place_ref[3]
    total = hide_ref.shape[1]
    row = lax.broadcasted_iota(jnp.int32, (block, 128), 0)
    lane = lax.broadcasted_iota(jnp.int32, (block, 128), 1)
    qseg = jnp.zeros((block, 128), jnp.int32)
    for a in range(8):
        first = (y * 16 + a * 2 + core) * block
        for i in range(block):
            qseg = jnp.where(lane == a * block + i, ids_ref[first + i], qseg)
    slot = lax.broadcasted_iota(jnp.int32, (total - block, 128), 0)
    for j in range(8):
        shard = ((y + 4 - j // 2) % 4) * 16 + z * 2 + (core if j % 2 == 0 else 1 - core)
        old = jnp.where(slot < lens_ref[shard], 0.0, HIDE).astype(jnp.bfloat16)
        kseg = jnp.zeros((block, 128), jnp.int32)
        for i in range(block):
            kseg = jnp.where(row == i, ids_ref[shard * block + i], kseg)
        new = jnp.where(kseg <= qseg, 0.0, HIDE).astype(jnp.bfloat16)
        hide_ref[j] = jnp.concatenate([old, new], axis=0)
    token = lax.broadcasted_iota(jnp.int32, pick_ref.shape, 0) // 8
    picked = token == lax.broadcasted_iota(jnp.int32, pick_ref.shape, 1)
    pick_ref[...] = jnp.where(picked, 1.0, 0.0).astype(jnp.bfloat16)


def prep(lens, ids, place, total):
    smem = pl.BlockSpec(memory_space=pltpu.SMEM)
    vmem = pl.BlockSpec(memory_space=pltpu.VMEM)
    return pl.pallas_call(
        prep_kernel,
        out_shape=(
            jax.ShapeDtypeStruct((8, total, 128), jnp.bfloat16),
            jax.ShapeDtypeStruct((1024, 128), jnp.bfloat16),
        ),
        in_specs=[smem, smem, smem],
        out_specs=(vmem, vmem),
        compiler_params=pltpu.CompilerParams(vmem_limit_bytes=8 << 20),
        name="prep",
    )(lens, ids, place)


def join_kernel(cache_ref, new_ref, out_ref):
    count = cache_ref.shape[1]
    for kind in range(2):
        out_ref[kind, 0:count, :] = cache_ref[kind]
        out_ref[kind, count : out_ref.shape[1], :] = new_ref[kind]


def join(cache, new):
    return pl.pallas_call(
        join_kernel,
        out_shape=jax.ShapeDtypeStruct((2, cache.shape[1] + new.shape[1], HEAD), cache.dtype),
        out_specs=pl.BlockSpec(memory_space=pltpu.VMEM),
        compiler_params=pltpu.CompilerParams(vmem_limit_bytes=4 << 20),
        name="join",
    )(cache, new)


def spread_kernel(q_ref, out_ref):
    for g in range(8):
        heads = []
        for r in range(2):
            for h in range(8):
                at = (g * 8 + h) * HEAD
                heads.append(q_ref[r : r + 1, at : at + HEAD])
        block = jnp.concatenate(heads, axis=0)
        for a in range(8):
            out_ref[a * 8 + g] = block


def spread(q):
    vmem = pl.BlockSpec(memory_space=pltpu.VMEM)
    return pl.pallas_call(
        spread_kernel,
        out_shape=jax.ShapeDtypeStruct((64, 16, HEAD), q.dtype),
        in_specs=[vmem],
        out_specs=vmem,
        compiler_params=pltpu.CompilerParams(vmem_limit_bytes=4 << 20),
        name="spread",
    )(q)


def pair_kernel(one_ref, two_ref, out_ref):
    out_ref[0] = one_ref[...]
    out_ref[1] = two_ref[...]


def pair(one, two):
    vmem = pl.BlockSpec(memory_space=pltpu.VMEM)
    return pl.pallas_call(
        pair_kernel,
        out_shape=jax.ShapeDtypeStruct((2, *one.shape), one.dtype),
        in_specs=[vmem, vmem],
        out_specs=vmem,
        compiler_params=pltpu.CompilerParams(vmem_limit_bytes=4 << 20),
        name="pair",
    )(one, two)


def attend_kernel(shards, chunks, has_state, final, *refs):
    q_ref, pick_ref, hide_ref = refs[:3]
    chunk_refs = []
    rest = list(refs[3:])
    for _ in range(chunks):
        ref = rest.pop(0)
        chunk_refs += [ref] if len(ref.shape) == 3 else [ref.at[0], ref.at[1]]
    state_ref = rest[0] if has_state else None
    out_ref, turned_ref = rest[-2:]
    rows = q_ref.shape[0]
    tile = 256
    scale = HEAD**-0.5
    factor = scale * math.log2(math.e)
    steps = [(part, which) for part in range(rows // tile) for which in range(len(shards))]

    def score(step):
        part, which = step
        cols = slice(part * tile, (part + 1) * tile)
        keys = jnp.concatenate([chunk_refs[which][0], hide_ref[shards[which]]], axis=1)
        q = jnp.concatenate([q_ref[cols, :], pick_ref[cols, :]], axis=1)
        return lax.dot_general(keys, q, (((1,), (1,)), ((), ())), preferred_element_type=jnp.float32)

    s = score(steps[0])
    for which in range(len(shards)):
        turned_ref[which] = chunk_refs[which][1].T
    acc = peak = denom = None
    for at, (part, which) in enumerate(steps):
        ahead = score(steps[at + 1]) if at + 1 < len(steps) else None
        cols = slice(part * tile, (part + 1) * tile)
        if which == 0:
            acc = peak = denom = None
            if has_state:
                acc = state_ref[0:HEAD, cols]
                peak = state_ref[HEAD : HEAD + 1, cols]
                denom = state_ref[HEAD + 1 : HEAD + 2, cols]
        m = jnp.max(s, axis=0, keepdims=True)
        e = jnp.exp2((s - m) * factor)
        l = jnp.sum(e, axis=0, keepdims=True)
        o = jnp.dot(turned_ref[which], e.astype(jnp.bfloat16), preferred_element_type=jnp.float32)
        if acc is None:
            acc, peak, denom = o, m, l
        else:
            top = jnp.maximum(peak, m)
            keep = jnp.exp2((peak - top) * factor)
            fresh = jnp.exp2((m - top) * factor)
            acc = acc * keep + o * fresh
            denom = denom * keep + l * fresh
            peak = top
        s = ahead
        if which + 1 < len(shards):
            continue
        if not final:
            out_ref[0:HEAD, cols] = acc
            out_ref[HEAD : HEAD + 1, cols] = peak
            out_ref[HEAD + 1 : HEAD + 2, cols] = denom
        else:
            acc = acc / denom
            lse = peak * scale + jnp.log(denom)
            for half in range(tile // 128):
                block = acc[:, half * 128 : (half + 1) * 128].T
                line = lse[:, half * 128 : (half + 1) * 128]
                for t in range(8):
                    to = ((part * (tile // 128) + half) * 8 + t) * 17
                    out_ref[to : to + 16, :] = block[t * 16 : (t + 1) * 16, :]
                    out_ref[to + 16 : to + 17, :] = line


def attend(shards, q, prepared, chunks, state=None, final=False):
    vmem = pl.BlockSpec(memory_space=pltpu.VMEM)
    hide, pick = prepared
    operands = [q, pick, hide, *chunks]
    aliases = {}
    shape = (1088, 128) if final else (HEAD + 8, q.shape[0])
    if state is not None:
        if not final:
            aliases = {len(operands): 0}
        operands.append(state)
    work = len(shards) * q.shape[0] * chunks[0].shape[-2]
    return pl.pallas_call(
        functools.partial(attend_kernel, tuple(shards), len(chunks), state is not None, final),
        out_shape=jax.ShapeDtypeStruct(shape, jnp.float32),
        in_specs=[vmem] * len(operands),
        out_specs=vmem,
        input_output_aliases=aliases,
        scratch_shapes=[pltpu.VMEM((len(shards), HEAD, chunks[0].shape[-2]), jnp.bfloat16)],
        cost_estimate=pl.CostEstimate(flops=4 * HEAD * work, transcendentals=work, bytes_accessed=1 << 20),
        compiler_params=pltpu.CompilerParams(vmem_limit_bytes=32 << 20),
        name="attend",
    )(*operands)


def combine_kernel(place_ref, got_ref, out_ref, lse_ref, turned_ref, line_ref):
    me = place_ref[0]
    lse = got_ref[pl.ds(16, 64, stride=17), :].reshape(8, 8, 128)
    peak = jnp.max(lse, axis=0)
    w = jnp.exp(lse - peak[None])
    denom = jnp.sum(w, axis=0)
    w = (w / denom[None]).reshape(64, 128)
    turned_ref[...] = jnp.concatenate([w, w], axis=0).T
    line_ref[...] = peak + jnp.log(denom)
    mine = turned_ref[pl.ds(pl.multiple_of(me * 16, 16), 16), :]
    for g in range(8):
        acc = None
        for z in range(8):
            at = z * 8 + g
            term = got_ref[at * 17 : at * 17 + 16, :] * mine[:, at : at + 1]
            acc = term if acc is None else acc + term
        for h in range(8):
            pair = jnp.concatenate([acc[h : h + 1], acc[8 + h : 9 + h]], axis=0)
            out_ref[:, (g * 8 + h) * 128 : (g * 8 + h + 1) * 128] = pair.astype(jnp.bfloat16)
    line = jnp.broadcast_to(line_ref[pl.ds(me, 1), :], (16, 128))
    row = lax.broadcasted_iota(jnp.int32, (16, 128), 0)
    table = line
    for i in range(1, 16):
        table = jnp.where(row == i, pltpu.roll(line, 128 - 8 * i, 1), table)
    table = jnp.concatenate([table] * 8, axis=0).T
    lse_ref[...] = table[:8, :16]


def combine(place, got):
    smem = pl.BlockSpec(memory_space=pltpu.SMEM)
    vmem = pl.BlockSpec(memory_space=pltpu.VMEM)
    return pl.pallas_call(
        combine_kernel,
        out_shape=(
            jax.ShapeDtypeStruct((2, 8192), jnp.bfloat16),
            jax.ShapeDtypeStruct((8, 16), jnp.float32),
        ),
        in_specs=[smem, vmem],
        out_specs=(vmem, vmem),
        scratch_shapes=[pltpu.VMEM((128, 128), jnp.float32), pltpu.VMEM((8, 128), jnp.float32)],
        compiler_params=pltpu.CompilerParams(vmem_limit_bytes=8 << 20),
        name="combine",
    )(place, got)


def shards_program(q_new, kv_new, kv_cache, cache_lens, segment_ids):
    y1, y0, z1, z0, core = (lax.axis_index(name) for name in CTX)
    place = jnp.stack([lax.axis_index(TP), y1 * 2 + y0, z1 * 2 + z0, core]).astype(jnp.int32)
    swap = [(0, 1), (1, 0)]

    own = join(kv_cache, kv_new)
    turn = lambda by: [(i, (i + by) % 4) for i in range(4)]
    one = lax.ppermute(own, ("y1", "y0"), turn(1))
    two = lax.ppermute(own, ("y1", "y0"), turn(2))
    three = lax.ppermute(own, ("y1", "y0"), turn(3))
    own_x = lax.ppermute(own, "core", swap)
    q = spread(q_new)
    q = lax.all_to_all(q, ROUTE, split_axis=0, concat_axis=0, tiled=True)
    q = q.reshape(1024, HEAD)
    prepared = prep(cache_lens, segment_ids, place, own.shape[1])
    two_x = lax.ppermute(two, "core", swap)
    both = pair(one, three)
    both_x = lax.ppermute(both, "core", swap)
    chunk = {0: own, 1: own_x, 2: one, 4: two, 6: three, 5: two_x, (3, 7): both_x, (2, 6): both}
    state = None
    for n, shards in enumerate(GROUPS):
        final = n + 1 == len(GROUPS)
        flat = [j for entry in shards for j in (entry if isinstance(entry, tuple) else (entry,))]
        state = attend(flat, q, prepared, [chunk[j] for j in shards], state, final=final)
    sent = state.reshape(64, 1, 2176)
    got = lax.all_to_all(sent, ROUTE, split_axis=0, concat_axis=0, tiled=True)
    out, lse = combine(place, got.reshape(1088, HEAD))
    return out, lse.T


GROUPS = [[0, 1], [4, 5], [(2, 6)], [(3, 7)]]


def solution(mesh):
    fine = Mesh(mesh.devices.reshape(2, 2, 4, 2, 2, 4, 2), CTX + TP)
    rows = P(CTX + TP, None)
    kv = P(None, CTX, TP)
    return jax.shard_map(
        shards_program,
        mesh=fine,
        in_specs=(rows, kv, kv, P(), P()),
        out_specs=(rows, P(CTX, TP)),
        check_vma=False,
    )
```

```python
import functools
import math

import jax
import jax.numpy as jnp
from jax import lax
from jax.experimental import pallas as pl
from jax.experimental.pallas import tpu as pltpu
from jax.sharding import Mesh
from jax.sharding import PartitionSpec as P


HEAD = 128
HIDE = -1e30
SENT = 10
CTX = ("y1", "y0", "z1", "z0", "core")
TP = ("x", "yl")
ROUTE = ("z1", "z0", "x", "yl")


def prep_kernel(lens_ref, ids_ref, place_ref, filled_ref, kseg_ref, qseg_ref, pick_ref):
    block = pick_ref.shape[0] // 64
    y, z, core = place_ref[1], place_ref[2], place_ref[3]
    row = lax.broadcasted_iota(jnp.int32, (block, 128), 0)
    lane = lax.broadcasted_iota(jnp.int32, (8, 128), 1)
    which = lax.broadcasted_iota(jnp.int32, (8, 128), 0)
    qseg = jnp.zeros((8, 128), jnp.int32)
    for a in range(8):
        first = (y * 16 + a * 2 + core) * block
        for i in range(block):
            qseg = jnp.where(lane == a * block + i, ids_ref[first + i], qseg)
    qseg_ref[...] = qseg
    filled = jnp.zeros((8, 128), jnp.int32)
    for j in range(8):
        shard = ((y + 4 - j // 2) % 4) * 16 + z * 2 + (core if j % 2 == 0 else 1 - core)
        filled = jnp.where(which == j, lens_ref[shard], filled)
        kseg = jnp.zeros((block, 128), jnp.int32)
        for i in range(block):
            kseg = jnp.where(row == i, ids_ref[shard * block + i], kseg)
        kseg_ref[j] = kseg
    filled_ref[...] = filled
    token = lax.broadcasted_iota(jnp.int32, pick_ref.shape, 0) // 8
    picked = token == lax.broadcasted_iota(jnp.int32, pick_ref.shape, 1)
    pick_ref[...] = jnp.where(picked, 1.0, 0.0).astype(jnp.bfloat16)


def prep(lens, ids, place):
    smem = pl.BlockSpec(memory_space=pltpu.SMEM)
    vmem = pl.BlockSpec(memory_space=pltpu.VMEM)
    return pl.pallas_call(
        prep_kernel,
        out_shape=(
            jax.ShapeDtypeStruct((8, 128), jnp.int32),
            jax.ShapeDtypeStruct((8, 16, 128), jnp.int32),
            jax.ShapeDtypeStruct((8, 128), jnp.int32),
            jax.ShapeDtypeStruct((1024, 128), jnp.bfloat16),
        ),
        in_specs=[smem, smem, smem],
        out_specs=(vmem, vmem, vmem, vmem),
        compiler_params=pltpu.CompilerParams(vmem_limit_bytes=4 << 20),
        name="prep",
    )(lens, ids, place)


def join_kernel(cache_ref, new_ref, out_ref):
    count = cache_ref.shape[1]
    for kind in range(2):
        out_ref[kind, 0:count, :] = cache_ref[kind]
        out_ref[kind, count : out_ref.shape[1], :] = new_ref[kind]


def join(cache, new):
    return pl.pallas_call(
        join_kernel,
        out_shape=jax.ShapeDtypeStruct((2, cache.shape[1] + new.shape[1], HEAD), cache.dtype),
        out_specs=pl.BlockSpec(memory_space=pltpu.VMEM),
        compiler_params=pltpu.CompilerParams(vmem_limit_bytes=4 << 20),
        name="join",
    )(cache, new)


def spread_kernel(q_ref, out_ref):
    for g in range(8):
        heads = []
        for r in range(2):
            for h in range(8):
                at = (g * 8 + h) * HEAD
                heads.append(q_ref[r : r + 1, at : at + HEAD])
        block = jnp.concatenate(heads, axis=0)
        for a in range(8):
            out_ref[a * 8 + g] = block


def spread(q):
    vmem = pl.BlockSpec(memory_space=pltpu.VMEM)
    return pl.pallas_call(
        spread_kernel,
        out_shape=jax.ShapeDtypeStruct((64, 16, HEAD), q.dtype),
        in_specs=[vmem],
        out_specs=vmem,
        compiler_params=pltpu.CompilerParams(vmem_limit_bytes=4 << 20),
        name="spread",
    )(q)


def pair_kernel(*refs):
    for n, ref in enumerate(refs[:-1]):
        refs[-1][n] = ref[...]


def pair(*chunks):
    vmem = pl.BlockSpec(memory_space=pltpu.VMEM)
    return pl.pallas_call(
        pair_kernel,
        out_shape=jax.ShapeDtypeStruct((len(chunks), *chunks[0].shape), chunks[0].dtype),
        in_specs=[vmem] * len(chunks),
        out_specs=vmem,
        compiler_params=pltpu.CompilerParams(vmem_limit_bytes=4 << 20),
        name="pair",
    )(*chunks)


def attend_kernel(shards, chunks, has_state, final, *refs):
    q_ref, filled_ref, kseg_ref, qseg_ref, pick_ref = refs[:5]
    chunk_refs = []
    rest = list(refs[5:])
    for _ in range(chunks):
        ref = rest.pop(0)
        chunk_refs += [ref] if len(ref.shape) == 3 else [ref.at[n] for n in range(ref.shape[0])]
    state_ref = rest[0] if has_state else None
    out_ref, turned_ref, hide_ref = rest[-3:]
    rows = q_ref.shape[0]
    tile = 256
    scale = HEAD**-0.5
    factor = scale * math.log2(math.e)
    steps = [(part, which) for part in range(rows // tile) for which in range(len(shards))]

    block = kseg_ref.shape[1]
    slot = lax.broadcasted_iota(jnp.int32, (hide_ref.shape[1] - block, HEAD), 0)
    for which, j in enumerate(shards):
        old = jnp.where(slot < filled_ref[j : j + 1, :], 0.0, HIDE).astype(jnp.bfloat16)
        new = jnp.where(kseg_ref[j] <= qseg_ref[0:1, :], 0.0, HIDE).astype(jnp.bfloat16)
        hide_ref[which] = jnp.concatenate([old, new], axis=0)

    def score(step):
        part, which = step
        cols = slice(part * tile, (part + 1) * tile)
        keys = jnp.concatenate([chunk_refs[which][0], hide_ref[which]], axis=1)
        q = jnp.concatenate([q_ref[cols, :], pick_ref[cols, :]], axis=1)
        return lax.dot_general(keys, q, (((1,), (1,)), ((), ())), preferred_element_type=jnp.float32)

    s = score(steps[0])
    for which in range(len(shards)):
        turned_ref[which] = chunk_refs[which][1].T
    acc = peak = denom = None
    for at, (part, which) in enumerate(steps):
        ahead = score(steps[at + 1]) if at + 1 < len(steps) else None
        cols = slice(part * tile, (part + 1) * tile)
        if which == 0:
            acc = peak = denom = None
            if has_state:
                acc = state_ref[0:HEAD, cols]
                peak = state_ref[HEAD : HEAD + 1, cols]
                denom = state_ref[HEAD + 1 : HEAD + 2, cols]
        m = jnp.max(s, axis=0, keepdims=True)
        e = jnp.exp2((s - m) * factor)
        l = jnp.sum(e, axis=0, keepdims=True)
        o = jnp.dot(turned_ref[which], e.astype(jnp.bfloat16), preferred_element_type=jnp.float32)
        if acc is None:
            acc, peak, denom = o, m, l
        else:
            top = jnp.maximum(peak, m)
            keep = jnp.exp2((peak - top) * factor)
            fresh = jnp.exp2((m - top) * factor)
            acc = acc * keep + o * fresh
            denom = denom * keep + l * fresh
            peak = top
        s = ahead
        if which + 1 < len(shards):
            continue
        if not final:
            out_ref[0:HEAD, cols] = acc
            out_ref[HEAD : HEAD + 1, cols] = peak
            out_ref[HEAD + 1 : HEAD + 2, cols] = denom
        else:
            size = jnp.max(jnp.abs(acc), axis=0, keepdims=True) / denom
            power = jnp.ceil(jnp.log2(jnp.maximum(size, 1e-33)) + 0.001)
            acc = jnp.floor(acc * (jnp.exp2(15.0 - power) / denom) + 0.5)
            lse = jnp.floor((peak * scale + jnp.log(denom)) * 65536.0 + 0.5).astype(jnp.int32)
            power = power.astype(jnp.int32)
            for half in range(tile // 128):
                lanes = slice(half * 128, (half + 1) * 128)
                block = acc[:, lanes].T.astype(jnp.int32)
                for t in range(8):
                    to = ((part * (tile // 128) + half) * 8 + t) * SENT
                    upper = block[t * 16 : t * 16 + 8, :]
                    lower = block[t * 16 + 8 : t * 16 + 16, :]
                    out_ref[to : to + 8, :] = (upper << 16) | (lower & 0xFFFF)
                    out_ref[to + 8 : to + 9, :] = lse[:, lanes]
                    out_ref[to + 9 : to + 10, :] = power[:, lanes]


def attend(shards, q, prepared, chunks, state=None, final=False):
    vmem = pl.BlockSpec(memory_space=pltpu.VMEM)
    operands = [q, *prepared, *chunks]
    aliases = {}
    shape = jax.ShapeDtypeStruct((HEAD + 8, q.shape[0]), jnp.float32)
    if final:
        shape = jax.ShapeDtypeStruct((64 * SENT, 128), jnp.int32)
    if state is not None:
        if not final:
            aliases = {len(operands): 0}
        operands.append(state)
    work = len(shards) * q.shape[0] * chunks[0].shape[-2]
    return pl.pallas_call(
        functools.partial(attend_kernel, tuple(shards), len(chunks), state is not None, final),
        out_shape=shape,
        in_specs=[vmem] * len(operands),
        out_specs=vmem,
        input_output_aliases=aliases,
        scratch_shapes=[
            pltpu.VMEM((len(shards), HEAD, chunks[0].shape[-2]), jnp.bfloat16),
            pltpu.VMEM((len(shards), chunks[0].shape[-2], HEAD), jnp.bfloat16),
        ],
        cost_estimate=pl.CostEstimate(flops=4 * HEAD * work, transcendentals=work, bytes_accessed=1 << 20),
        compiler_params=pltpu.CompilerParams(vmem_limit_bytes=16 << 20),
        name="attend",
    )(*operands)


def combine_kernel(place_ref, got_ref, out_ref, lse_ref, turned_ref, line_ref):
    me = place_ref[0]
    lse = got_ref[pl.ds(8, 64, stride=SENT), :].astype(jnp.float32) * (1.0 / 65536.0)
    power = got_ref[pl.ds(9, 64, stride=SENT), :].astype(jnp.float32) - 15.0
    lse = lse.reshape(8, 8, 128)
    peak = jnp.max(lse, axis=0)
    w = jnp.exp(lse - peak[None])
    denom = jnp.sum(w, axis=0)
    w = (w / denom[None]).reshape(64, 128) * jnp.exp2(power)
    turned_ref[...] = jnp.concatenate([w, w], axis=0).T
    line_ref[...] = peak + jnp.log(denom)
    mine = turned_ref[pl.ds(pl.multiple_of(me * 16, 16), 16), :]
    for g in range(8):
        tops = bottoms = None
        for a in range(8):
            at = a * 8 + g
            word = got_ref[at * SENT : at * SENT + 8, :]
            top = (word >> 16).astype(jnp.float32) * mine[:8, at : at + 1]
            bottom = ((word << 16) >> 16).astype(jnp.float32) * mine[8:, at : at + 1]
            tops = top if tops is None else tops + top
            bottoms = bottom if bottoms is None else bottoms + bottom
        for h in range(8):
            rows = jnp.concatenate([tops[h : h + 1], bottoms[h : h + 1]], axis=0)
            out_ref[:, (g * 8 + h) * HEAD : (g * 8 + h + 1) * HEAD] = rows.astype(jnp.bfloat16)
    line = jnp.broadcast_to(line_ref[pl.ds(me, 1), :], (16, 128))
    row = lax.broadcasted_iota(jnp.int32, (16, 128), 0)
    table = line
    for i in range(1, 16):
        table = jnp.where(row == i, pltpu.roll(line, 128 - 8 * i, 1), table)
    table = jnp.concatenate([table] * 8, axis=0).T
    lse_ref[...] = table[:8, :16]


def combine(place, got):
    smem = pl.BlockSpec(memory_space=pltpu.SMEM)
    vmem = pl.BlockSpec(memory_space=pltpu.VMEM)
    return pl.pallas_call(
        combine_kernel,
        out_shape=(
            jax.ShapeDtypeStruct((2, 8192), jnp.bfloat16),
            jax.ShapeDtypeStruct((8, 16), jnp.float32),
        ),
        in_specs=[smem, vmem],
        out_specs=(vmem, vmem),
        scratch_shapes=[pltpu.VMEM((128, 128), jnp.float32), pltpu.VMEM((8, 128), jnp.float32)],
        compiler_params=pltpu.CompilerParams(vmem_limit_bytes=8 << 20),
        name="combine",
    )(place, got)


def shards_program(q_new, kv_new, kv_cache, cache_lens, segment_ids):
    y1, y0, z1, z0, core = (lax.axis_index(name) for name in CTX)
    place = jnp.stack([lax.axis_index(TP), y1 * 2 + y0, z1 * 2 + z0, core]).astype(jnp.int32)
    swap = [(0, 1), (1, 0)]

    own = join(kv_cache, kv_new)
    turn = lambda by: [(i, (i + by) % 4) for i in range(4)]
    one = lax.ppermute(own, ("y1", "y0"), turn(1))
    three = lax.ppermute(own, ("y1", "y0"), turn(3))
    two = lax.ppermute(one, ("y1", "y0"), turn(1))
    q = spread(q_new)
    q = lax.all_to_all(q, ROUTE, split_axis=0, concat_axis=0, tiled=True)
    q = q.reshape(1024, HEAD)
    prepared = prep(cache_lens, segment_ids, place)
    both0 = pair(own, one, three)
    sent0 = lax.ppermute(both0, "core", swap)
    sent1 = lax.ppermute(two, "core", swap)
    chunk = {0: own, 2: one, 4: two, 6: three, (1, 3, 7): sent0, (0, 2, 6): both0, 5: sent1}
    state = None
    for n, shards in enumerate(GROUPS):
        final = n + 1 == len(GROUPS)
        flat = [j for entry in shards for j in (entry if isinstance(entry, tuple) else (entry,))]
        state = attend(flat, q, prepared, [chunk[j] for j in shards], state, final=final)
    sent = state.reshape(64, 1, SENT * 128)
    got = lax.all_to_all(sent, ROUTE, split_axis=0, concat_axis=0, tiled=True)
    out, lse = combine(place, got.reshape(64 * SENT, 128))
    return out, lse.T


GROUPS = [[(0, 2, 6)], [(1, 3, 7)], [4], [5]]


def solution(mesh):
    fine = Mesh(mesh.devices.reshape(2, 2, 4, 2, 2, 4, 2), CTX + TP)
    rows = P(CTX + TP, None)
    kv = P(None, CTX, TP)
    return jax.shard_map(
        shards_program,
        mesh=fine,
        in_specs=(rows, kv, kv, P(), P()),
        out_specs=(rows, P(CTX, TP)),
        check_vma=False,
    )
```

```python
import functools
import math

import jax
import jax.numpy as jnp
from jax import lax
from jax.experimental import pallas as pl
from jax.experimental.pallas import tpu as pltpu
from jax.sharding import Mesh
from jax.sharding import PartitionSpec as P


HEAD = 128
HIDE = -1e30
SENT = 10
CTX = ("y1", "y0", "z1", "z0", "core")
TP = ("x", "yl")
ROUTE = ("z1", "z0", "x", "yl")


def prep_kernel(lens_ref, ids_ref, place_ref, filled_ref, kseg_ref, qseg_ref, pick_ref):
    block = pick_ref.shape[0] // 64
    y, z, core = place_ref[1], place_ref[2], place_ref[3]
    row = lax.broadcasted_iota(jnp.int32, (block, 128), 0)
    lane = lax.broadcasted_iota(jnp.int32, (8, 128), 1)
    which = lax.broadcasted_iota(jnp.int32, (8, 128), 0)
    qseg = jnp.zeros((8, 128), jnp.int32)
    for a in range(8):
        first = (y * 16 + a * 2 + core) * block
        for i in range(block):
            qseg = jnp.where(lane == a * block + i, ids_ref[first + i], qseg)
    qseg_ref[...] = qseg
    filled = jnp.zeros((8, 128), jnp.int32)
    for j in range(8):
        side = core if j % 2 == 0 else 1 - core
        step = j // 2
        shard = ((y + 4 - step + 2 * step * side) % 4) * 16 + z * 2 + side
        filled = jnp.where(which == j, lens_ref[shard], filled)
        kseg = jnp.zeros((block, 128), jnp.int32)
        for i in range(block):
            kseg = jnp.where(row == i, ids_ref[shard * block + i], kseg)
        kseg_ref[j] = kseg
    filled_ref[...] = filled
    token = lax.broadcasted_iota(jnp.int32, pick_ref.shape, 0) // 8
    picked = token == lax.broadcasted_iota(jnp.int32, pick_ref.shape, 1)
    pick_ref[...] = jnp.where(picked, 1.0, 0.0).astype(jnp.bfloat16)


def prep(lens, ids, place):
    smem = pl.BlockSpec(memory_space=pltpu.SMEM)
    vmem = pl.BlockSpec(memory_space=pltpu.VMEM)
    return pl.pallas_call(
        prep_kernel,
        out_shape=(
            jax.ShapeDtypeStruct((8, 128), jnp.int32),
            jax.ShapeDtypeStruct((8, 16, 128), jnp.int32),
            jax.ShapeDtypeStruct((8, 128), jnp.int32),
            jax.ShapeDtypeStruct((1024, 128), jnp.bfloat16),
        ),
        in_specs=[smem, smem, smem],
        out_specs=(vmem, vmem, vmem, vmem),
        compiler_params=pltpu.CompilerParams(vmem_limit_bytes=4 << 20),
        name="prep",
    )(lens, ids, place)


def join_kernel(cache_ref, new_ref, out_ref):
    count = cache_ref.shape[1]
    for kind in range(2):
        out_ref[kind, 0:count, :] = cache_ref[kind]
        out_ref[kind, count : out_ref.shape[1], :] = new_ref[kind]


def join(cache, new):
    return pl.pallas_call(
        join_kernel,
        out_shape=jax.ShapeDtypeStruct((2, cache.shape[1] + new.shape[1], HEAD), cache.dtype),
        out_specs=pl.BlockSpec(memory_space=pltpu.VMEM),
        compiler_params=pltpu.CompilerParams(vmem_limit_bytes=4 << 20),
        name="join",
    )(cache, new)


def spread_kernel(q_ref, out_ref):
    for g in range(8):
        heads = []
        for r in range(2):
            for h in range(8):
                at = (g * 8 + h) * HEAD
                heads.append(q_ref[r : r + 1, at : at + HEAD])
        block = jnp.concatenate(heads, axis=0)
        for a in range(8):
            out_ref[a * 8 + g] = block


def spread(q):
    vmem = pl.BlockSpec(memory_space=pltpu.VMEM)
    return pl.pallas_call(
        spread_kernel,
        out_shape=jax.ShapeDtypeStruct((64, 16, HEAD), q.dtype),
        in_specs=[vmem],
        out_specs=vmem,
        compiler_params=pltpu.CompilerParams(vmem_limit_bytes=4 << 20),
        name="spread",
    )(q)


def pair_kernel(*refs):
    for n, ref in enumerate(refs[:-1]):
        refs[-1][n] = ref[...]


def pair(*chunks):
    vmem = pl.BlockSpec(memory_space=pltpu.VMEM)
    return pl.pallas_call(
        pair_kernel,
        out_shape=jax.ShapeDtypeStruct((len(chunks), *chunks[0].shape), chunks[0].dtype),
        in_specs=[vmem] * len(chunks),
        out_specs=vmem,
        compiler_params=pltpu.CompilerParams(vmem_limit_bytes=4 << 20),
        name="pair",
    )(*chunks)


def attend_kernel(shards, chunks, has_state, final, *refs):
    q_ref, filled_ref, kseg_ref, qseg_ref, pick_ref = refs[:5]
    chunk_refs = []
    rest = list(refs[5:])
    for _ in range(chunks):
        ref = rest.pop(0)
        chunk_refs += [ref] if len(ref.shape) == 3 else [ref.at[n] for n in range(ref.shape[0])]
    state_ref = rest[0] if has_state else None
    out_ref, turned_ref, hide_ref = rest[-3:]
    rows = q_ref.shape[0]
    tile = 256
    scale = HEAD**-0.5
    factor = scale * math.log2(math.e)
    steps = [(part, which) for part in range(rows // tile) for which in range(len(shards))]

    block = kseg_ref.shape[1]
    slot = lax.broadcasted_iota(jnp.int32, (hide_ref.shape[1] - block, HEAD), 0)
    for which, j in enumerate(shards):
        old = jnp.where(slot < filled_ref[j : j + 1, :], 0.0, HIDE).astype(jnp.bfloat16)
        new = jnp.where(kseg_ref[j] <= qseg_ref[0:1, :], 0.0, HIDE).astype(jnp.bfloat16)
        hide_ref[which] = jnp.concatenate([old, new], axis=0)

    def score(step):
        part, which = step
        cols = slice(part * tile, (part + 1) * tile)
        keys = jnp.concatenate([chunk_refs[which][0], hide_ref[which]], axis=1)
        q = jnp.concatenate([q_ref[cols, :], pick_ref[cols, :]], axis=1)
        return lax.dot_general(keys, q, (((1,), (1,)), ((), ())), preferred_element_type=jnp.float32)

    s = score(steps[0])
    for which in range(len(shards)):
        turned_ref[which] = chunk_refs[which][1].T
    acc = peak = denom = None
    for at, (part, which) in enumerate(steps):
        ahead = score(steps[at + 1]) if at + 1 < len(steps) else None
        cols = slice(part * tile, (part + 1) * tile)
        if which == 0:
            acc = peak = denom = None
            if has_state:
                acc = state_ref[0:HEAD, cols]
                peak = state_ref[HEAD : HEAD + 1, cols]
                denom = state_ref[HEAD + 1 : HEAD + 2, cols]
        m = jnp.max(s, axis=0, keepdims=True)
        e = jnp.exp2((s - m) * factor)
        l = jnp.sum(e, axis=0, keepdims=True)
        o = jnp.dot(turned_ref[which], e.astype(jnp.bfloat16), preferred_element_type=jnp.float32)
        if acc is None:
            acc, peak, denom = o, m, l
        else:
            top = jnp.maximum(peak, m)
            keep = jnp.exp2((peak - top) * factor)
            fresh = jnp.exp2((m - top) * factor)
            acc = acc * keep + o * fresh
            denom = denom * keep + l * fresh
            peak = top
        s = ahead
        if which + 1 < len(shards):
            continue
        if not final:
            out_ref[0:HEAD, cols] = acc
            out_ref[HEAD : HEAD + 1, cols] = peak
            out_ref[HEAD + 1 : HEAD + 2, cols] = denom
        else:
            size = jnp.max(jnp.abs(acc), axis=0, keepdims=True) / denom
            power = jnp.ceil(jnp.log2(jnp.maximum(size, 1e-33)) + 0.001)
            acc = jnp.floor(acc * (jnp.exp2(15.0 - power) / denom) + 0.5)
            lse = jnp.floor((peak * scale + jnp.log(denom)) * 65536.0 + 0.5).astype(jnp.int32)
            power = power.astype(jnp.int32)
            for half in range(tile // 128):
                lanes = slice(half * 128, (half + 1) * 128)
                block = acc[:, lanes].T.astype(jnp.int32)
                for t in range(8):
                    to = ((part * (tile // 128) + half) * 8 + t) * SENT
                    upper = block[t * 16 : t * 16 + 8, :]
                    lower = block[t * 16 + 8 : t * 16 + 16, :]
                    out_ref[to : to + 8, :] = (upper << 16) | (lower & 0xFFFF)
                    out_ref[to + 8 : to + 9, :] = lse[:, lanes]
                    out_ref[to + 9 : to + 10, :] = power[:, lanes]


def attend(shards, q, prepared, chunks, state=None, final=False):
    vmem = pl.BlockSpec(memory_space=pltpu.VMEM)
    operands = [q, *prepared, *chunks]
    aliases = {}
    shape = jax.ShapeDtypeStruct((HEAD + 8, q.shape[0]), jnp.float32)
    if final:
        shape = jax.ShapeDtypeStruct((64 * SENT, 128), jnp.int32)
    if state is not None:
        if not final:
            aliases = {len(operands): 0}
        operands.append(state)
    work = len(shards) * q.shape[0] * chunks[0].shape[-2]
    return pl.pallas_call(
        functools.partial(attend_kernel, tuple(shards), len(chunks), state is not None, final),
        out_shape=shape,
        in_specs=[vmem] * len(operands),
        out_specs=vmem,
        input_output_aliases=aliases,
        scratch_shapes=[
            pltpu.VMEM((len(shards), HEAD, chunks[0].shape[-2]), jnp.bfloat16),
            pltpu.VMEM((len(shards), chunks[0].shape[-2], HEAD), jnp.bfloat16),
        ],
        cost_estimate=pl.CostEstimate(flops=4 * HEAD * work, transcendentals=work, bytes_accessed=1 << 20),
        compiler_params=pltpu.CompilerParams(vmem_limit_bytes=16 << 20),
        name="attend",
    )(*operands)


def combine_kernel(got_ref, out_ref, lse_ref, turned_ref, line_ref):
    me = lax.axis_index("x") * 2 + lax.axis_index("yl")
    lse = got_ref[pl.ds(8, 64, stride=SENT), :].astype(jnp.float32) * (1.0 / 65536.0)
    power = got_ref[pl.ds(9, 64, stride=SENT), :].astype(jnp.float32) - 15.0
    lse = lse.reshape(8, 8, 128)
    peak = jnp.max(lse, axis=0)
    w = jnp.exp(lse - peak[None])
    denom = jnp.sum(w, axis=0)
    w = (w / denom[None]).reshape(64, 128) * jnp.exp2(power)
    turned_ref[...] = jnp.concatenate([w, w], axis=0).T
    line_ref[...] = peak + jnp.log(denom)
    mine = turned_ref[pl.ds(pl.multiple_of(me * 16, 16), 16), :]
    for g in range(8):
        tops = bottoms = None
        for a in range(8):
            at = a * 8 + g
            word = got_ref[at * SENT : at * SENT + 8, :]
            top = (word >> 16).astype(jnp.float32) * mine[:8, at : at + 1]
            bottom = ((word << 16) >> 16).astype(jnp.float32) * mine[8:, at : at + 1]
            tops = top if tops is None else tops + top
            bottoms = bottom if bottoms is None else bottoms + bottom
        for h in range(8):
            rows = jnp.concatenate([tops[h : h + 1], bottoms[h : h + 1]], axis=0)
            out_ref[:, (g * 8 + h) * HEAD : (g * 8 + h + 1) * HEAD] = rows.astype(jnp.bfloat16)
    line = jnp.broadcast_to(line_ref[pl.ds(me, 1), :], (16, 128))
    row = lax.broadcasted_iota(jnp.int32, (16, 128), 0)
    table = line
    for i in range(1, 16):
        table = jnp.where(row == i, pltpu.roll(line, 128 - 8 * i, 1), table)
    table = jnp.concatenate([table] * 8, axis=0).T
    lse_ref[...] = table[:8, :16]


def combine(got):
    vmem = pl.BlockSpec(memory_space=pltpu.VMEM)
    return pl.pallas_call(
        combine_kernel,
        out_shape=(
            jax.ShapeDtypeStruct((2, 8192), jnp.bfloat16),
            jax.ShapeDtypeStruct((8, 16), jnp.float32),
        ),
        in_specs=[vmem],
        out_specs=(vmem, vmem),
        scratch_shapes=[pltpu.VMEM((128, 128), jnp.float32), pltpu.VMEM((8, 128), jnp.float32)],
        compiler_params=pltpu.CompilerParams(vmem_limit_bytes=8 << 20),
        name="combine",
    )(got)


def shards_program(q_new, kv_new, kv_cache, cache_lens, segment_ids):
    y1, y0, z1, z0, core = (lax.axis_index(name) for name in CTX)
    place = jnp.stack([lax.axis_index(TP), y1 * 2 + y0, z1 * 2 + z0, core]).astype(jnp.int32)
    swap = [(0, 1), (1, 0)]

    own = join(kv_cache, kv_new)
    turn = lambda by: [(i * 2 + c, (i + (4 - by if c else by)) % 4 * 2 + c) for i in range(4) for c in range(2)]
    ring = ("y1", "y0", "core")
    one = lax.ppermute(own, ring, turn(1))
    three = lax.ppermute(own, ring, turn(3))
    two = lax.ppermute(one, ring, turn(1))
    q = spread(q_new)
    q = lax.all_to_all(q, ROUTE, split_axis=0, concat_axis=0, tiled=True)
    q = q.reshape(1024, HEAD)
    prepared = prep(cache_lens, segment_ids, place)
    both0 = pair(own, one, three)
    sent0 = lax.ppermute(both0, "core", swap)
    sent1 = lax.ppermute(two, "core", swap)
    chunk = {0: own, 2: one, 4: two, 6: three, (1, 3, 7): sent0, (0, 2, 6): both0, 5: sent1}
    state = None
    for n, shards in enumerate(GROUPS):
        final = n + 1 == len(GROUPS)
        flat = [j for entry in shards for j in (entry if isinstance(entry, tuple) else (entry,))]
        state = attend(flat, q, prepared, [chunk[j] for j in shards], state, final=final)
    sent = state.reshape(64, 1, SENT * 128)
    got = lax.all_to_all(sent, ROUTE, split_axis=0, concat_axis=0, tiled=True)
    out, lse = combine(got.reshape(64 * SENT, 128))
    return out, lse.T


GROUPS = [[(0, 2, 6)], [(1, 3, 7)], [4], [5]]


def solution(mesh):
    fine = Mesh(mesh.devices.reshape(2, 2, 4, 2, 2, 4, 2), CTX + TP)
    rows = P(CTX + TP, None)
    kv = P(None, CTX, TP)
    return jax.shard_map(
        shards_program,
        mesh=fine,
        in_specs=(rows, kv, kv, P(), P()),
        out_specs=(rows, P(CTX, TP)),
        check_vma=False,
    )
```

```python
import functools
import math

import jax
import jax.numpy as jnp
from jax import lax
from jax.experimental import pallas as pl
from jax.experimental.pallas import tpu as pltpu
from jax.sharding import Mesh
from jax.sharding import PartitionSpec as P


HEAD = 128
HIDE = -1e30
SENT = 10
CTX = ("y1", "y0", "z1", "z0", "core")
TP = ("x", "yl")
ROUTE = ("z1", "z0", "x", "yl")


def prep_kernel(lens_ref, ids_ref, filled_ref, kseg_ref, qseg_ref, pick_ref):
    block = pick_ref.shape[0] // 64
    y = lax.axis_index("y1") * 2 + lax.axis_index("y0")
    z = lax.axis_index("z1") * 2 + lax.axis_index("z0")
    core = lax.axis_index("core")
    row = lax.broadcasted_iota(jnp.int32, (block, 128), 0)
    lane = lax.broadcasted_iota(jnp.int32, (8, 128), 1)
    which = lax.broadcasted_iota(jnp.int32, (8, 128), 0)
    qseg = jnp.zeros((8, 128), jnp.int32)
    for a in range(8):
        first = (y * 16 + a * 2 + core) * block
        for i in range(block):
            qseg = jnp.where(lane == a * block + i, ids_ref[first + i], qseg)
    qseg_ref[...] = qseg
    filled = jnp.zeros((8, 128), jnp.int32)
    for j in range(8):
        side = core if j % 2 == 0 else 1 - core
        step = j // 2
        shard = ((y + 4 - step + 2 * step * side) % 4) * 16 + z * 2 + side
        filled = jnp.where(which == j, lens_ref[shard], filled)
        kseg = jnp.zeros((block, 128), jnp.int32)
        for i in range(block):
            kseg = jnp.where(row == i, ids_ref[shard * block + i], kseg)
        kseg_ref[j] = kseg
    filled_ref[...] = filled
    token = lax.broadcasted_iota(jnp.int32, pick_ref.shape, 0) // 8
    picked = token == lax.broadcasted_iota(jnp.int32, pick_ref.shape, 1)
    pick_ref[...] = jnp.where(picked, 1.0, 0.0).astype(jnp.bfloat16)


def prep(lens, ids):
    smem = pl.BlockSpec(memory_space=pltpu.SMEM)
    vmem = pl.BlockSpec(memory_space=pltpu.VMEM)
    return pl.pallas_call(
        prep_kernel,
        out_shape=(
            jax.ShapeDtypeStruct((8, 128), jnp.int32),
            jax.ShapeDtypeStruct((8, 16, 128), jnp.int32),
            jax.ShapeDtypeStruct((8, 128), jnp.int32),
            jax.ShapeDtypeStruct((1024, 128), jnp.bfloat16),
        ),
        in_specs=[smem, smem],
        out_specs=(vmem, vmem, vmem, vmem),
        compiler_params=pltpu.CompilerParams(vmem_limit_bytes=4 << 20),
        name="prep",
    )(lens, ids)


def join_kernel(cache_ref, new_ref, out_ref):
    count = cache_ref.shape[1]
    for kind in range(2):
        out_ref[kind, 0:count, :] = cache_ref[kind]
        out_ref[kind, count : out_ref.shape[1], :] = new_ref[kind]


def join(cache, new):
    return pl.pallas_call(
        join_kernel,
        out_shape=jax.ShapeDtypeStruct((2, cache.shape[1] + new.shape[1], HEAD), cache.dtype),
        out_specs=pl.BlockSpec(memory_space=pltpu.VMEM),
        compiler_params=pltpu.CompilerParams(vmem_limit_bytes=4 << 20),
        name="join",
    )(cache, new)


def spread_kernel(q_ref, out_ref):
    for g in range(8):
        heads = []
        for r in range(2):
            for h in range(8):
                at = (g * 8 + h) * HEAD
                heads.append(q_ref[r : r + 1, at : at + HEAD])
        block = jnp.concatenate(heads, axis=0)
        for a in range(8):
            out_ref[a * 8 + g] = block


def spread(q):
    vmem = pl.BlockSpec(memory_space=pltpu.VMEM)
    return pl.pallas_call(
        spread_kernel,
        out_shape=jax.ShapeDtypeStruct((64, 16, HEAD), q.dtype),
        in_specs=[vmem],
        out_specs=vmem,
        compiler_params=pltpu.CompilerParams(vmem_limit_bytes=4 << 20),
        name="spread",
    )(q)


def pair_kernel(*refs):
    for n, ref in enumerate(refs[:-1]):
        refs[-1][n] = ref[...]


def pair(*chunks):
    vmem = pl.BlockSpec(memory_space=pltpu.VMEM)
    return pl.pallas_call(
        pair_kernel,
        out_shape=jax.ShapeDtypeStruct((len(chunks), *chunks[0].shape), chunks[0].dtype),
        in_specs=[vmem] * len(chunks),
        out_specs=vmem,
        compiler_params=pltpu.CompilerParams(vmem_limit_bytes=4 << 20),
        name="pair",
    )(*chunks)


def attend_kernel(shards, chunks, has_state, final, *refs):
    q_ref, filled_ref, kseg_ref, qseg_ref, pick_ref = refs[:5]
    chunk_refs = []
    rest = list(refs[5:])
    for _ in range(chunks):
        ref = rest.pop(0)
        chunk_refs += [ref] if len(ref.shape) == 3 else [ref.at[n] for n in range(ref.shape[0])]
    state_ref = rest[0] if has_state else None
    out_ref, turned_ref, hide_ref = rest[-3:]
    rows = q_ref.shape[0]
    tile = 256 if final else 512
    scale = HEAD**-0.5
    factor = scale * math.log2(math.e)
    steps = [(part, which) for part in range(rows // tile) for which in range(len(shards))]

    block = kseg_ref.shape[1]
    slot = lax.broadcasted_iota(jnp.int32, (hide_ref.shape[1] - block, HEAD), 0)
    for which, j in enumerate(shards):
        old = jnp.where(slot < filled_ref[j : j + 1, :], 0.0, HIDE).astype(jnp.bfloat16)
        new = jnp.where(kseg_ref[j] <= qseg_ref[0:1, :], 0.0, HIDE).astype(jnp.bfloat16)
        hide_ref[which] = jnp.concatenate([old, new], axis=0)

    def score(step):
        part, which = step
        cols = slice(part * tile, (part + 1) * tile)
        keys = jnp.concatenate([chunk_refs[which][0], hide_ref[which]], axis=1)
        q = jnp.concatenate([q_ref[cols, :], pick_ref[cols, :]], axis=1)
        return lax.dot_general(keys, q, (((1,), (1,)), ((), ())), preferred_element_type=jnp.float32)

    s = score(steps[0])
    for which in range(len(shards)):
        turned_ref[which] = chunk_refs[which][1].T
    acc = peak = denom = None
    for at, (part, which) in enumerate(steps):
        ahead = score(steps[at + 1]) if at + 1 < len(steps) else None
        cols = slice(part * tile, (part + 1) * tile)
        if which == 0:
            acc = peak = denom = None
            if has_state:
                acc = state_ref[0:HEAD, cols]
                peak = state_ref[HEAD : HEAD + 1, cols]
                denom = state_ref[HEAD + 1 : HEAD + 2, cols]
        m = jnp.max(s, axis=0, keepdims=True)
        e = jnp.exp2((s - m) * factor)
        l = jnp.sum(e, axis=0, keepdims=True)
        o = jnp.dot(turned_ref[which], e.astype(jnp.bfloat16), preferred_element_type=jnp.float32)
        if acc is None:
            acc, peak, denom = o, m, l
        else:
            top = jnp.maximum(peak, m)
            keep = jnp.exp2((peak - top) * factor)
            fresh = jnp.exp2((m - top) * factor)
            acc = acc * keep + o * fresh
            denom = denom * keep + l * fresh
            peak = top
        s = ahead
        if which + 1 < len(shards):
            continue
        if not final:
            out_ref[0:HEAD, cols] = acc
            out_ref[HEAD : HEAD + 1, cols] = peak
            out_ref[HEAD + 1 : HEAD + 2, cols] = denom
        else:
            size = jnp.max(jnp.abs(acc), axis=0, keepdims=True) / denom
            power = jnp.ceil(jnp.log2(jnp.maximum(size, 1e-33)) + 0.001)
            acc = jnp.floor(acc * (jnp.exp2(15.0 - power) / denom) + 0.5)
            lse = jnp.floor((peak * scale + jnp.log(denom)) * 65536.0 + 0.5).astype(jnp.int32)
            power = power.astype(jnp.int32)
            for half in range(tile // 128):
                lanes = slice(half * 128, (half + 1) * 128)
                block = acc[:, lanes].T.astype(jnp.int32)
                for t in range(8):
                    to = ((part * (tile // 128) + half) * 8 + t) * SENT
                    upper = block[t * 16 : t * 16 + 8, :]
                    lower = block[t * 16 + 8 : t * 16 + 16, :]
                    out_ref[to : to + 8, :] = (upper << 16) | (lower & 0xFFFF)
                    out_ref[to + 8 : to + 9, :] = lse[:, lanes]
                    out_ref[to + 9 : to + 10, :] = power[:, lanes]


def attend(shards, q, prepared, chunks, state=None, final=False):
    vmem = pl.BlockSpec(memory_space=pltpu.VMEM)
    operands = [q, *prepared, *chunks]
    aliases = {}
    shape = jax.ShapeDtypeStruct((HEAD + 8, q.shape[0]), jnp.float32)
    if final:
        shape = jax.ShapeDtypeStruct((64 * SENT, 128), jnp.int32)
    if state is not None:
        if not final:
            aliases = {len(operands): 0}
        operands.append(state)
    work = len(shards) * q.shape[0] * chunks[0].shape[-2]
    return pl.pallas_call(
        functools.partial(attend_kernel, tuple(shards), len(chunks), state is not None, final),
        out_shape=shape,
        in_specs=[vmem] * len(operands),
        out_specs=vmem,
        input_output_aliases=aliases,
        scratch_shapes=[
            pltpu.VMEM((len(shards), HEAD, chunks[0].shape[-2]), jnp.bfloat16),
            pltpu.VMEM((len(shards), chunks[0].shape[-2], HEAD), jnp.bfloat16),
        ],
        cost_estimate=pl.CostEstimate(flops=4 * HEAD * work, transcendentals=work, bytes_accessed=1 << 20),
        compiler_params=pltpu.CompilerParams(vmem_limit_bytes=16 << 20),
        name="attend",
    )(*operands)


def combine_kernel(got_ref, out_ref, lse_ref, turned_ref, line_ref):
    me = lax.axis_index("x") * 2 + lax.axis_index("yl")
    lse = got_ref[pl.ds(8, 64, stride=SENT), :].astype(jnp.float32) * (1.0 / 65536.0)
    power = got_ref[pl.ds(9, 64, stride=SENT), :].astype(jnp.float32) - 15.0
    lse = lse.reshape(8, 8, 128)
    peak = jnp.max(lse, axis=0)
    w = jnp.exp(lse - peak[None])
    denom = jnp.sum(w, axis=0)
    w = (w / denom[None]).reshape(64, 128) * jnp.exp2(power)
    turned_ref[...] = jnp.concatenate([w, w], axis=0).T
    line_ref[...] = peak + jnp.log(denom)
    mine = turned_ref[pl.ds(pl.multiple_of(me * 16, 16), 16), :]
    for g in range(8):
        tops = bottoms = None
        for a in range(8):
            at = a * 8 + g
            word = got_ref[at * SENT : at * SENT + 8, :]
            top = (word >> 16).astype(jnp.float32) * mine[:8, at : at + 1]
            bottom = ((word << 16) >> 16).astype(jnp.float32) * mine[8:, at : at + 1]
            tops = top if tops is None else tops + top
            bottoms = bottom if bottoms is None else bottoms + bottom
        for h in range(8):
            rows = jnp.concatenate([tops[h : h + 1], bottoms[h : h + 1]], axis=0)
            out_ref[:, (g * 8 + h) * HEAD : (g * 8 + h + 1) * HEAD] = rows.astype(jnp.bfloat16)
    line = jnp.broadcast_to(line_ref[pl.ds(me, 1), :], (16, 128))
    row = lax.broadcasted_iota(jnp.int32, (16, 128), 0)
    table = line
    for i in range(1, 16):
        table = jnp.where(row == i, pltpu.roll(line, 128 - 8 * i, 1), table)
    table = jnp.concatenate([table] * 8, axis=0).T
    lse_ref[...] = table[:8, :16]


def combine(got):
    vmem = pl.BlockSpec(memory_space=pltpu.VMEM)
    return pl.pallas_call(
        combine_kernel,
        out_shape=(
            jax.ShapeDtypeStruct((2, 8192), jnp.bfloat16),
            jax.ShapeDtypeStruct((8, 16), jnp.float32),
        ),
        in_specs=[vmem],
        out_specs=(vmem, vmem),
        scratch_shapes=[pltpu.VMEM((128, 128), jnp.float32), pltpu.VMEM((8, 128), jnp.float32)],
        compiler_params=pltpu.CompilerParams(vmem_limit_bytes=8 << 20),
        name="combine",
    )(got)


def shards_program(q_new, kv_new, kv_cache, cache_lens, segment_ids):
    swap = [(0, 1), (1, 0)]

    own = join(kv_cache, kv_new)
    turn = lambda by: [(i * 2 + c, (i + (4 - by if c else by)) % 4 * 2 + c) for i in range(4) for c in range(2)]
    ring = ("y1", "y0", "core")
    one = lax.ppermute(own, ring, turn(1))
    three = lax.ppermute(own, ring, turn(3))
    two = lax.ppermute(one, ring, turn(1))
    q = spread(q_new)
    q = lax.all_to_all(q, ROUTE, split_axis=0, concat_axis=0, tiled=True)
    q = q.reshape(1024, HEAD)
    prepared = prep(cache_lens, segment_ids)
    both0 = pair(own, one, three)
    sent0 = lax.ppermute(both0, "core", swap)
    sent1 = lax.ppermute(two, "core", swap)
    chunk = {0: own, 2: one, 4: two, 6: three, (1, 3, 7): sent0, (0, 2, 6): both0, 5: sent1}
    state = None
    for n, shards in enumerate(GROUPS):
        final = n + 1 == len(GROUPS)
        flat = [j for entry in shards for j in (entry if isinstance(entry, tuple) else (entry,))]
        state = attend(flat, q, prepared, [chunk[j] for j in shards], state, final=final)
    sent = state.reshape(64, 1, SENT * 128)
    got = lax.all_to_all(sent, ROUTE, split_axis=0, concat_axis=0, tiled=True)
    out, lse = combine(got.reshape(64 * SENT, 128))
    return out, lse.T


GROUPS = [[(0, 2, 6)], [(1, 3, 7)], [4], [5]]


def solution(mesh):
    fine = Mesh(mesh.devices.reshape(2, 2, 4, 2, 2, 4, 2), CTX + TP)
    rows = P(CTX + TP, None)
    kv = P(None, CTX, TP)
    return jax.shard_map(
        shards_program,
        mesh=fine,
        in_specs=(rows, kv, kv, P(), P()),
        out_specs=(rows, P(CTX, TP)),
        check_vma=False,
    )
```

```python
import functools
import math

import jax
import jax.numpy as jnp
from jax import lax
from jax.experimental import pallas as pl
from jax.experimental.pallas import tpu as pltpu
from jax.sharding import Mesh
from jax.sharding import PartitionSpec as P


HEAD = 128
HIDE = -1e30
SENT = 10
CTX = ("y1", "y0", "z1", "z0", "core")
TP = ("x", "yl")
ROUTE = ("z1", "z0", "x", "yl")
BACK = ("x", "yl", "z1", "z0")


def prep_kernel(lens_ref, ids_ref, filled_ref, kseg_ref, qseg_ref, pick_ref):
    block = pick_ref.shape[0] // 64
    y = lax.axis_index("y1") * 2 + lax.axis_index("y0")
    z = lax.axis_index("z1") * 2 + lax.axis_index("z0")
    core = lax.axis_index("core")
    row = lax.broadcasted_iota(jnp.int32, (block, 128), 0)
    lane = lax.broadcasted_iota(jnp.int32, (8, 128), 1)
    which = lax.broadcasted_iota(jnp.int32, (8, 128), 0)
    qseg = jnp.zeros((8, 128), jnp.int32)
    for a in range(8):
        first = (y * 16 + a * 2 + core) * block
        for i in range(block):
            qseg = jnp.where(lane == a * block + i, ids_ref[first + i], qseg)
    qseg_ref[...] = qseg
    filled = jnp.zeros((8, 128), jnp.int32)
    for j in range(8):
        side = core if j % 2 == 0 else 1 - core
        step = j // 2
        shard = ((y + 4 - step + 2 * step * side) % 4) * 16 + z * 2 + side
        filled = jnp.where(which == j, lens_ref[shard], filled)
        kseg = jnp.zeros((block, 128), jnp.int32)
        for i in range(block):
            kseg = jnp.where(row == i, ids_ref[shard * block + i], kseg)
        kseg_ref[j] = kseg
    filled_ref[...] = filled
    token = lax.broadcasted_iota(jnp.int32, pick_ref.shape, 0) // 8
    picked = token == lax.broadcasted_iota(jnp.int32, pick_ref.shape, 1)
    pick_ref[...] = jnp.where(picked, 1.0, 0.0).astype(jnp.bfloat16)


def prep(lens, ids):
    smem = pl.BlockSpec(memory_space=pltpu.SMEM)
    vmem = pl.BlockSpec(memory_space=pltpu.VMEM)
    return pl.pallas_call(
        prep_kernel,
        out_shape=(
            jax.ShapeDtypeStruct((8, 128), jnp.int32),
            jax.ShapeDtypeStruct((8, 16, 128), jnp.int32),
            jax.ShapeDtypeStruct((8, 128), jnp.int32),
            jax.ShapeDtypeStruct((1024, 128), jnp.bfloat16),
        ),
        in_specs=[smem, smem],
        out_specs=(vmem, vmem, vmem, vmem),
        compiler_params=pltpu.CompilerParams(vmem_limit_bytes=4 << 20),
        name="prep",
    )(lens, ids)


def join_kernel(cache_ref, new_ref, out_ref):
    count = cache_ref.shape[1]
    for kind in range(2):
        out_ref[kind, 0:count, :] = cache_ref[kind]
        out_ref[kind, count : out_ref.shape[1], :] = new_ref[kind]


def join(cache, new):
    return pl.pallas_call(
        join_kernel,
        out_shape=jax.ShapeDtypeStruct((2, cache.shape[1] + new.shape[1], HEAD), cache.dtype),
        out_specs=pl.BlockSpec(memory_space=pltpu.VMEM),
        compiler_params=pltpu.CompilerParams(vmem_limit_bytes=4 << 20),
        name="join",
    )(cache, new)


def spread_kernel(q_ref, out_ref):
    for g in range(8):
        heads = []
        for r in range(2):
            for h in range(8):
                at = (g * 8 + h) * HEAD
                heads.append(q_ref[r : r + 1, at : at + HEAD])
        block = jnp.concatenate(heads, axis=0)
        for a in range(8):
            out_ref[a * 8 + g] = block


def spread(q):
    vmem = pl.BlockSpec(memory_space=pltpu.VMEM)
    return pl.pallas_call(
        spread_kernel,
        out_shape=jax.ShapeDtypeStruct((64, 16, HEAD), q.dtype),
        in_specs=[vmem],
        out_specs=vmem,
        compiler_params=pltpu.CompilerParams(vmem_limit_bytes=4 << 20),
        name="spread",
    )(q)


def pair_kernel(*refs):
    for n, ref in enumerate(refs[:-1]):
        refs[-1][n] = ref[...]


def pair(*chunks):
    vmem = pl.BlockSpec(memory_space=pltpu.VMEM)
    return pl.pallas_call(
        pair_kernel,
        out_shape=jax.ShapeDtypeStruct((len(chunks), *chunks[0].shape), chunks[0].dtype),
        in_specs=[vmem] * len(chunks),
        out_specs=vmem,
        compiler_params=pltpu.CompilerParams(vmem_limit_bytes=4 << 20),
        name="pair",
    )(*chunks)


def attend_kernel(shards, chunks, has_state, final, *refs):
    q_ref, filled_ref, kseg_ref, qseg_ref, pick_ref = refs[:5]
    chunk_refs = []
    rest = list(refs[5:])
    for _ in range(chunks):
        ref = rest.pop(0)
        chunk_refs += [ref] if len(ref.shape) == 3 else [ref.at[n] for n in range(ref.shape[0])]
    state_ref = rest[0] if has_state else None
    out_ref, turned_ref, hide_ref = rest[-3:]
    rows = q_ref.shape[0]
    tile = 256 if final else 512
    scale = HEAD**-0.5
    factor = scale * math.log2(math.e)
    steps = [(part, which) for part in range(rows // tile) for which in range(len(shards))]

    block = kseg_ref.shape[1]
    slot = lax.broadcasted_iota(jnp.int32, (hide_ref.shape[1] - block, HEAD), 0)
    for which, j in enumerate(shards):
        old = jnp.where(slot < filled_ref[j : j + 1, :], 0.0, HIDE).astype(jnp.bfloat16)
        new = jnp.where(kseg_ref[j] <= qseg_ref[0:1, :], 0.0, HIDE).astype(jnp.bfloat16)
        hide_ref[which] = jnp.concatenate([old, new], axis=0)

    def score(step):
        part, which = step
        cols = slice(part * tile, (part + 1) * tile)
        keys = jnp.concatenate([chunk_refs[which][0], hide_ref[which]], axis=1)
        q = jnp.concatenate([q_ref[cols, :], pick_ref[cols, :]], axis=1)
        return lax.dot_general(keys, q, (((1,), (1,)), ((), ())), preferred_element_type=jnp.float32)

    s = score(steps[0])
    for which in range(len(shards)):
        turned_ref[which] = chunk_refs[which][1].T
    acc = peak = denom = None
    for at, (part, which) in enumerate(steps):
        ahead = score(steps[at + 1]) if at + 1 < len(steps) else None
        cols = slice(part * tile, (part + 1) * tile)
        if which == 0:
            acc = peak = denom = None
            if has_state:
                acc = state_ref[0:HEAD, cols]
                peak = state_ref[HEAD : HEAD + 1, cols]
                denom = state_ref[HEAD + 1 : HEAD + 2, cols]
        m = jnp.max(s, axis=0, keepdims=True)
        e = jnp.exp2((s - m) * factor)
        l = jnp.sum(e, axis=0, keepdims=True)
        o = jnp.dot(turned_ref[which], e.astype(jnp.bfloat16), preferred_element_type=jnp.float32)
        if acc is None:
            acc, peak, denom = o, m, l
        else:
            top = jnp.maximum(peak, m)
            keep = jnp.exp2((peak - top) * factor)
            fresh = jnp.exp2((m - top) * factor)
            acc = acc * keep + o * fresh
            denom = denom * keep + l * fresh
            peak = top
        s = ahead
        if which + 1 < len(shards):
            continue
        if not final:
            out_ref[0:HEAD, cols] = acc
            out_ref[HEAD : HEAD + 1, cols] = peak
            out_ref[HEAD + 1 : HEAD + 2, cols] = denom
        else:
            size = jnp.max(jnp.abs(acc), axis=0, keepdims=True) / denom
            power = jnp.ceil(jnp.log2(jnp.maximum(size, 1e-33)) + 0.001)
            acc = jnp.floor(acc * (jnp.exp2(15.0 - power) / denom) + 0.5)
            lse = jnp.floor((peak * scale + jnp.log(denom)) * 65536.0 + 0.5).astype(jnp.int32)
            power = power.astype(jnp.int32)
            for half in range(tile // 128):
                lanes = slice(half * 128, (half + 1) * 128)
                block = acc[:, lanes].T.astype(jnp.int32)
                for t in range(8):
                    to = (t * 8 + part * (tile // 128) + half) * SENT
                    upper = block[t * 16 : t * 16 + 8, :]
                    lower = block[t * 16 + 8 : t * 16 + 16, :]
                    out_ref[to : to + 8, :] = (upper << 16) | (lower & 0xFFFF)
                    out_ref[to + 8 : to + 9, :] = lse[:, lanes]
                    out_ref[to + 9 : to + 10, :] = power[:, lanes]


def attend(shards, q, prepared, chunks, state=None, final=False):
    vmem = pl.BlockSpec(memory_space=pltpu.VMEM)
    operands = [q, *prepared, *chunks]
    aliases = {}
    shape = jax.ShapeDtypeStruct((HEAD + 8, q.shape[0]), jnp.float32)
    if final:
        shape = jax.ShapeDtypeStruct((64 * SENT, 128), jnp.int32)
    if state is not None:
        if not final:
            aliases = {len(operands): 0}
        operands.append(state)
    work = len(shards) * q.shape[0] * chunks[0].shape[-2]
    return pl.pallas_call(
        functools.partial(attend_kernel, tuple(shards), len(chunks), state is not None, final),
        out_shape=shape,
        in_specs=[vmem] * len(operands),
        out_specs=vmem,
        input_output_aliases=aliases,
        scratch_shapes=[
            pltpu.VMEM((len(shards), HEAD, chunks[0].shape[-2]), jnp.bfloat16),
            pltpu.VMEM((len(shards), chunks[0].shape[-2], HEAD), jnp.bfloat16),
        ],
        cost_estimate=pl.CostEstimate(flops=4 * HEAD * work, transcendentals=work, bytes_accessed=1 << 20),
        compiler_params=pltpu.CompilerParams(vmem_limit_bytes=16 << 20),
        name="attend",
    )(*operands)


def combine_kernel(got_ref, out_ref, lse_ref, turned_ref, line_ref):
    me = lax.axis_index("x") * 2 + lax.axis_index("yl")
    lse = got_ref[pl.ds(8, 64, stride=SENT), :].astype(jnp.float32) * (1.0 / 65536.0)
    power = got_ref[pl.ds(9, 64, stride=SENT), :].astype(jnp.float32) - 15.0
    lse = lse.reshape(8, 8, 128)
    peak = jnp.max(lse, axis=1)
    w = jnp.exp(lse - peak[:, None])
    denom = jnp.sum(w, axis=1)
    w = (w / denom[:, None]).reshape(64, 128) * jnp.exp2(power)
    turned_ref[...] = jnp.concatenate([w, w], axis=0).T
    line_ref[...] = peak + jnp.log(denom)
    mine = turned_ref[pl.ds(pl.multiple_of(me * 16, 16), 16), :]
    for g in range(8):
        tops = bottoms = None
        for a in range(8):
            at = g * 8 + a
            word = got_ref[at * SENT : at * SENT + 8, :]
            top = (word >> 16).astype(jnp.float32) * mine[:8, at : at + 1]
            bottom = ((word << 16) >> 16).astype(jnp.float32) * mine[8:, at : at + 1]
            tops = top if tops is None else tops + top
            bottoms = bottom if bottoms is None else bottoms + bottom
        for h in range(8):
            rows = jnp.concatenate([tops[h : h + 1], bottoms[h : h + 1]], axis=0)
            out_ref[:, (g * 8 + h) * HEAD : (g * 8 + h + 1) * HEAD] = rows.astype(jnp.bfloat16)
    line = jnp.broadcast_to(line_ref[pl.ds(me, 1), :], (16, 128))
    row = lax.broadcasted_iota(jnp.int32, (16, 128), 0)
    table = line
    for i in range(1, 16):
        table = jnp.where(row == i, pltpu.roll(line, 128 - 8 * i, 1), table)
    table = jnp.concatenate([table] * 8, axis=0).T
    lse_ref[...] = table[:8, :16]


def combine(got):
    vmem = pl.BlockSpec(memory_space=pltpu.VMEM)
    return pl.pallas_call(
        combine_kernel,
        out_shape=(
            jax.ShapeDtypeStruct((2, 8192), jnp.bfloat16),
            jax.ShapeDtypeStruct((8, 16), jnp.float32),
        ),
        in_specs=[vmem],
        out_specs=(vmem, vmem),
        scratch_shapes=[pltpu.VMEM((128, 128), jnp.float32), pltpu.VMEM((8, 128), jnp.float32)],
        compiler_params=pltpu.CompilerParams(vmem_limit_bytes=8 << 20),
        name="combine",
    )(got)


def shards_program(q_new, kv_new, kv_cache, cache_lens, segment_ids):
    swap = [(0, 1), (1, 0)]

    own = join(kv_cache, kv_new)
    turn = lambda by: [(i * 2 + c, (i + (4 - by if c else by)) % 4 * 2 + c) for i in range(4) for c in range(2)]
    ring = ("y1", "y0", "core")
    one = lax.ppermute(own, ring, turn(1))
    three = lax.ppermute(own, ring, turn(3))
    two = lax.ppermute(one, ring, turn(1))
    q = spread(q_new)
    q = lax.all_to_all(q, ROUTE, split_axis=0, concat_axis=0, tiled=True)
    q = q.reshape(1024, HEAD)
    prepared = prep(cache_lens, segment_ids)
    both0 = pair(own, one, three)
    sent0 = lax.ppermute(both0, "core", swap)
    sent1 = lax.ppermute(two, "core", swap)
    chunk = {0: own, 2: one, 4: two, 6: three, (1, 3, 7): sent0, (0, 2, 6): both0, 5: sent1}
    state = None
    for n, shards in enumerate(GROUPS):
        final = n + 1 == len(GROUPS)
        flat = [j for entry in shards for j in (entry if isinstance(entry, tuple) else (entry,))]
        state = attend(flat, q, prepared, [chunk[j] for j in shards], state, final=final)
    sent = state.reshape(64, 1, SENT * 128)
    got = lax.all_to_all(sent, BACK, split_axis=0, concat_axis=0, tiled=True)
    out, lse = combine(got.reshape(64 * SENT, 128))
    return out, lse.T


GROUPS = [[(0, 2, 6)], [(1, 3, 7)], [4], [5]]


def solution(mesh):
    fine = Mesh(mesh.devices.reshape(2, 2, 4, 2, 2, 4, 2), CTX + TP)
    rows = P(CTX + TP, None)
    kv = P(None, CTX, TP)
    return jax.shard_map(
        shards_program,
        mesh=fine,
        in_specs=(rows, kv, kv, P(), P()),
        out_specs=(rows, P(CTX, TP)),
        check_vma=False,
    )
```
